32 devices in a mesh: section: 8 (over z, x), dp: 4 (over y, core).
Axes of the slice: x: 2, y: 2, z: 4, core: 2. Of those that a mesh axis runs over, the one named last changes fastest.
Arguments:
- block_arguments: bfloat16 [2, 4, 1024, 2048], P(None, 'dp', 'section'), may hold values from -6 to 6
- incoming_batches: bfloat16 [2, 4, 128, 2048], P(None, 'dp'), may hold values from -6 to 6
- output_adjoints: bfloat16 [2, 4, 1024, 2048], P(None, 'dp', 'section'), may hold values from -0.125 to 0.125
- objective_adjoints: bfloat16 [2, 4, 128, 2048], P(None, 'dp'), may hold values from -0.125 to 0.125
- kept_block_arguments: bfloat16 [2, 2, 4, 1024, 2048], P(None, None, 'dp', 'section'), may hold values from -6 to 6
- parameter_arrays: bfloat16 [8, 2048, 1536], P('section', 'dp'), may hold values from -0.125 to 0.125
Outputs:
- ahead_out: bfloat16 [2, 4, 1024, 2048], P(None, 'dp', 'section')
- section_grads: float32 [8, 2048, 1536], P('section', 'dp')
The draws below stay inside these ranges and needn't reach their ends.
All inputs are finite; a program needn't handle non-finite values.
Results may differ from the reference program's by a relative error of at most 0.013.
Values may be sent and summed in bfloat16 or wider, within the bound.
A program may use at most 128 MiB of HBM per device.

```python
import jax
import jax.numpy as jnp
from jax import lax

HIDDEN_FEATURES = 2048
FF = 512
SMALL_BATCH_SPAN = 128
GRAD_ROWS = 2048
N_SECTION = 8
N_DP = 4


def block_scale(rng, dims, pieces, low, largest):
    level, own = 1.0, jax.random.fold_in(rng, 6)
    for dim, parts in pieces:
        steps = jnp.exp(jax.random.uniform(jax.random.fold_in(own, dim), (parts,), jnp.float32, low / len(pieces), largest / len(pieces)))
        level = level * jnp.repeat(steps, dims[dim] // parts).reshape([-1 if axis == dim else 1 for axis in range(len(dims))])
    return level


def gaussian(stream_key, extent, width, limit, shards=(), held_as=jnp.bfloat16):
    drawn = width * jax.random.normal(stream_key, extent, jnp.float32)
    if shards:
        drawn = drawn * block_scale(stream_key, extent, shards, -0.22, 0.18)
    return jnp.clip(drawn, -limit, limit).astype(held_as)


def setup_inputs(seed: int = 0) -> dict:
    arg_keys = jax.random.split(jax.random.key(seed), 7)
    block_arguments = gaussian(arg_keys[0], (2, N_DP, N_SECTION * SMALL_BATCH_SPAN, HIDDEN_FEATURES), 1.0, 6.0, ((1, 4), (2, 8)))
    incoming_batches = gaussian(arg_keys[1], (2, N_DP, SMALL_BATCH_SPAN, HIDDEN_FEATURES), 1.0, 6.0, ((1, 4),))
    output_adjoints = gaussian(arg_keys[2], (2, N_DP, N_SECTION * SMALL_BATCH_SPAN, HIDDEN_FEATURES), (1.0 / GRAD_ROWS ** 0.5), 0.125, ((1, 4), (2, 8)))
    objective_adjoints = gaussian(arg_keys[3], (2, N_DP, SMALL_BATCH_SPAN, HIDDEN_FEATURES), (1.0 / GRAD_ROWS ** 0.5), 0.125, ((1, 4),))
    kept_block_arguments = gaussian(arg_keys[4], (2, 2, N_DP, N_SECTION * SMALL_BATCH_SPAN, HIDDEN_FEATURES), 1.0, 6.0, ((2, 4), (3, 8)))
    parameter_arrays = gaussian(arg_keys[5], (N_SECTION, HIDDEN_FEATURES, 3 * FF), HIDDEN_FEATURES ** -0.5, 0.125, ((0, 8), (1, 4)))
    return {"block_arguments": block_arguments, "incoming_batches": incoming_batches, "output_adjoints": output_adjoints, "objective_adjoints": objective_adjoints, "kept_block_arguments": kept_block_arguments, "parameter_arrays": parameter_arrays}


def normalize(row_block):
    values = row_block.astype(jnp.float32)
    inverse = lax.rsqrt(lax.optimization_barrier(jnp.mean(values * values, axis=-1, keepdims=True)) + 1e-06)
    return (values, inverse, (values * inverse).astype(jnp.bfloat16))

def section_forward(row_block, matrix):
    hidden_width = matrix.shape[1] // 3
    values, inverse, normed = normalize(row_block)
    projected = jnp.dot(normed, matrix[:, :2 * hidden_width], preferred_element_type=jnp.float32)
    gate_part = projected[:, :hidden_width]
    up_part = projected[:, hidden_width:]
    hidden = (gate_part * jax.nn.sigmoid(gate_part) * up_part).astype(jnp.bfloat16)
    branch = lax.dot_general(hidden, matrix[:, 2 * hidden_width:], (((1,), (1,)), ((), ())), preferred_element_type=jnp.float32)
    return (values + branch).astype(jnp.bfloat16)

def section_reverse_pass(row_block, cotangent, matrix, with_input):
    hidden_width = matrix.shape[1] // 3
    values, inverse, normed = normalize(row_block)
    projected = jnp.dot(normed, matrix[:, :2 * hidden_width], preferred_element_type=jnp.float32)
    gate_part = projected[:, :hidden_width]
    up_part = projected[:, hidden_width:]
    sigmoid_gate = jax.nn.sigmoid(gate_part)
    silu_gate = gate_part * sigmoid_gate
    hidden = (silu_gate * up_part).astype(jnp.bfloat16)
    hidden_grad = jnp.dot(cotangent, matrix[:, 2 * hidden_width:], preferred_element_type=jnp.float32)
    projected_grad = jnp.concatenate([hidden_grad * up_part * sigmoid_gate * (1.0 + gate_part * (1.0 - sigmoid_gate)), hidden_grad * silu_gate], axis=1).astype(jnp.bfloat16)
    inward_grad = lax.dot_general(normed, projected_grad, (((0,), (0,)), ((), ())), preferred_element_type=jnp.float32)
    outward_grad = lax.dot_general(cotangent, hidden, (((0,), (0,)), ((), ())), preferred_element_type=jnp.float32)
    weight_term = jnp.concatenate([inward_grad, outward_grad], axis=1)
    if not with_input:
        return (weight_term, None)
    normed_grad = lax.dot_general(projected_grad, matrix[:, :2 * hidden_width], (((1,), (1,)), ((), ())), preferred_element_type=jnp.float32)
    inner_sum = lax.optimization_barrier(jnp.mean(normed_grad * values, axis=-1, keepdims=True))
    input_grad = cotangent.astype(jnp.float32) + inverse * normed_grad - values * inverse * inverse * inverse * inner_sum
    return (weight_term, input_grad.astype(jnp.bfloat16))

def replica_sums(first_rows, first_cot, second_rows, second_cot, matrix):

    def add_one(total, items):
        rows_one, cot_one, rows_two, cot_two = items
        term_one, discarded_value = section_reverse_pass(rows_one, cot_one, matrix, False)
        term_two, discarded_second = section_reverse_pass(rows_two, cot_two, matrix, False)
        rounded = lax.optimization_barrier((term_one + term_two).astype(jnp.bfloat16))
        return (total + rounded.astype(jnp.float32), None)
    start = jnp.zeros((HIDDEN_FEATURES, 3 * FF), jnp.float32)
    total, discarded_value = lax.scan(add_one, start, (first_rows, first_cot, second_rows, second_cot))
    return total

def reference(block_arguments, incoming_batches, output_adjoints, objective_adjoints, kept_block_arguments, parameter_arrays):
    segment_sequence_catalog = N_SECTION
    first_in = block_arguments.reshape(2, N_DP, segment_sequence_catalog, SMALL_BATCH_SPAN, HIDDEN_FEATURES)
    first_cot = output_adjoints.reshape(2, N_DP, segment_sequence_catalog, SMALL_BATCH_SPAN, HIDDEN_FEATURES)
    retained_intermediates = kept_block_arguments.reshape(2, 2, N_DP, segment_sequence_catalog, SMALL_BATCH_SPAN, HIDDEN_FEATURES)
    matrices = jnp.stack([parameter_arrays, parameter_arrays[::-1]])

    def flatten_rows(rows):
        return rows.reshape(N_DP * SMALL_BATCH_SPAN, HIDDEN_FEATURES)

    def shaped(rows):
        return rows.reshape(N_DP, SMALL_BATCH_SPAN, HIDDEN_FEATURES)

    def first_pass(position):
        forward_list = []
        back_list = []
        for course in range(2):
            matrix = matrices[course, position]
            forward_list.append(shaped(section_forward(flatten_rows(first_in[course, :, position]), matrix)))
            discarded_value, back_rows = section_reverse_pass(flatten_rows(retained_intermediates[course, 0, :, position]), flatten_rows(first_cot[course, :, position]), matrix, True)
            back_list.append(shaped(back_rows))
        return (jnp.stack(forward_list), jnp.stack(back_list))
    first_out, returned = lax.map(first_pass, jnp.arange(segment_sequence_catalog))
    down_in = jnp.concatenate([incoming_batches[0][None], first_out[:-1, 0]], axis=0)
    up_in = jnp.concatenate([first_out[1:, 1], incoming_batches[1][None]], axis=0)
    descending_adjoint = jnp.concatenate([returned[1:, 0], objective_adjoints[0][None]], axis=0)
    ascending_adjoint = jnp.concatenate([objective_adjoints[1][None], returned[:-1, 1]], axis=0)
    second_in = jnp.stack([down_in, up_in], axis=1)
    second_cot = jnp.stack([descending_adjoint, ascending_adjoint], axis=1)

    def second_pass(position):
        forward_list = []
        sum_list = []
        for course in range(2):
            matrix = matrices[course, position]
            forward_list.append(shaped(section_forward(flatten_rows(second_in[position, course]), matrix)))
            sum_list.append(replica_sums(retained_intermediates[course, 0, :, position], first_cot[course, :, position], retained_intermediates[course, 1, :, position], second_cot[position, course], matrix))
        return (jnp.stack(forward_list), jnp.stack(sum_list))
    later_out, totals = lax.map(second_pass, jnp.arange(segment_sequence_catalog))
    section_grads = totals[:, 0] + totals[::-1, 1]
    ahead_out = jnp.transpose(later_out, (1, 2, 0, 3, 4)).reshape(2, N_DP, segment_sequence_catalog * SMALL_BATCH_SPAN, HIDDEN_FEATURES)
    return (ahead_out, section_grads)
```

```python
import jax
import jax.numpy as jnp
from jax import lax
from jax.sharding import PartitionSpec as P


def mirrored(block, axis):
    count = lax.axis_size(axis)
    return lax.ppermute(block, axis, [(i, count - 1 - i) for i in range(count)])


def passed_along(block, axis, distance):
    devices = range(lax.axis_size(axis))
    route = [(i - distance, i) for i in devices if i - distance in devices]
    return lax.ppermute(block, axis, route)


def normalize(row_block):
    values = row_block.astype(jnp.float32)
    inverse = lax.rsqrt(jnp.mean(values * values, axis=-1, keepdims=True) + 1e-06)
    return (values, inverse, (values * inverse).astype(jnp.bfloat16))


def section_forward(row_block, matrix):
    hidden_width = matrix.shape[1] // 3
    values, inverse, normed = normalize(row_block)
    projected = jnp.dot(normed, matrix[:, : 2 * hidden_width], preferred_element_type=jnp.float32)
    gate_part = projected[:, :hidden_width]
    up_part = projected[:, hidden_width:]
    hidden = (gate_part * jax.nn.sigmoid(gate_part) * up_part).astype(jnp.bfloat16)
    branch = lax.dot_general(
        hidden,
        matrix[:, 2 * hidden_width :],
        (((1,), (1,)), ((), ())),
        preferred_element_type=jnp.float32,
    )
    return (values + branch).astype(jnp.bfloat16)


def reverse_parts(row_block, cotangent, matrix, with_input):
    hidden_width = matrix.shape[1] // 3
    values, inverse, normed = normalize(row_block)
    projected = jnp.dot(normed, matrix[:, : 2 * hidden_width], preferred_element_type=jnp.float32)
    gate_part = projected[:, :hidden_width]
    up_part = projected[:, hidden_width:]
    sigmoid_gate = jax.nn.sigmoid(gate_part)
    silu_gate = gate_part * sigmoid_gate
    hidden = (silu_gate * up_part).astype(jnp.bfloat16)
    hidden_grad = jnp.dot(
        cotangent, matrix[:, 2 * hidden_width :], preferred_element_type=jnp.float32
    )
    projected_grad = jnp.concatenate(
        [
            hidden_grad * up_part * sigmoid_gate * (1.0 + gate_part * (1.0 - sigmoid_gate)),
            hidden_grad * silu_gate,
        ],
        axis=1,
    ).astype(jnp.bfloat16)
    pieces = (normed, projected_grad, cotangent, hidden)
    if not with_input:
        return (pieces, None)
    normed_grad = lax.dot_general(
        projected_grad,
        matrix[:, : 2 * hidden_width],
        (((1,), (1,)), ((), ())),
        preferred_element_type=jnp.float32,
    )
    inner_sum = jnp.mean(normed_grad * values, axis=-1, keepdims=True)
    input_grad = (
        cotangent.astype(jnp.float32)
        + inverse * normed_grad
        - values * inverse * inverse * inverse * inner_sum
    )
    return (pieces, input_grad.astype(jnp.bfloat16))


def weight_pieces(piece_list):
    normed = jnp.concatenate([item[0] for item in piece_list], axis=0)
    projected_grad = jnp.concatenate([item[1] for item in piece_list], axis=0)
    cotangent = jnp.concatenate([item[2] for item in piece_list], axis=0)
    hidden = jnp.concatenate([item[3] for item in piece_list], axis=0)
    inward_grad = lax.dot_general(
        normed, projected_grad, (((0,), (0,)), ((), ())), preferred_element_type=jnp.float32
    )
    outward_grad = lax.dot_general(
        cotangent, hidden, (((0,), (0,)), ((), ())), preferred_element_type=jnp.float32
    )
    return (inward_grad, outward_grad)


def on_device(
    block_arguments,
    incoming_batches,
    output_adjoints,
    objective_adjoints,
    kept_block_arguments,
    parameter_arrays,
):
    position = lax.axis_index("section")
    segment_sequence_catalog = lax.axis_size("section")
    own_slice = parameter_arrays[0]
    resident_parameter_array = lax.all_gather(own_slice, "dp", axis=0, tiled=True)
    first_section = position == 0
    last_section = position == segment_sequence_catalog - 1
    up_input = mirrored(block_arguments[1, 0], "section")
    up_first_rows = mirrored(kept_block_arguments[1, 0, 0], "section")
    up_first_cot = mirrored(output_adjoints[1, 0], "section")
    up_second_rows = mirrored(kept_block_arguments[1, 1, 0], "section")
    down_ahead = section_forward(block_arguments[0, 0], resident_parameter_array)
    up_ahead = section_forward(up_input, resident_parameter_array)
    down_first_parts, down_backward_flow = reverse_parts(
        kept_block_arguments[0, 0, 0], output_adjoints[0, 0], resident_parameter_array, True
    )
    upward_first_parts, upward_backward_flow = reverse_parts(
        up_first_rows, up_first_cot, resident_parameter_array, True
    )
    arrivals = [passed_along(item, "section", 1) for item in (down_ahead, up_ahead)]
    returns = [
        passed_along(item, "section", -1) for item in (down_backward_flow, upward_backward_flow)
    ]
    down_next = jnp.where(first_section, incoming_batches[0, 0], arrivals[0])
    up_next = jnp.where(first_section, incoming_batches[1, 0], arrivals[1])
    descending_adjoint = jnp.where(last_section, objective_adjoints[0, 0], returns[0])
    ascending_adjoint = jnp.where(last_section, objective_adjoints[1, 0], returns[1])
    down_out = section_forward(down_next, resident_parameter_array)
    up_out = section_forward(up_next, resident_parameter_array)
    down_second_parts, discarded_value = reverse_parts(
        kept_block_arguments[0, 1, 0], descending_adjoint, resident_parameter_array, False
    )
    upward_second_parts, discarded_second = reverse_parts(
        up_second_rows, ascending_adjoint, resident_parameter_array, False
    )
    inward_grad, outward_grad = weight_pieces(
        [down_first_parts, down_second_parts, upward_first_parts, upward_second_parts]
    )
    inward_sum, outward_sum = (
        lax.psum_scatter(
            inward_grad.astype(jnp.bfloat16), "dp", scatter_dimension=0, tiled=True
        ).astype(jnp.float32),
        lax.psum_scatter(
            outward_grad.astype(jnp.bfloat16), "dp", scatter_dimension=0, tiled=True
        ).astype(jnp.float32),
    )
    up_out = mirrored(up_out, "section")
    ahead_out = jnp.stack([down_out, up_out])[:, None]
    return (ahead_out, jnp.concatenate([inward_sum, outward_sum], axis=1)[None])


def solution(mesh):
    in_specs = (
        P(None, "dp", "section", None),
        P(None, "dp", None, None),
        P(None, "dp", "section", None),
        P(None, "dp", None, None),
        P(None, None, "dp", "section", None),
        P("section", "dp", None),
    )
    out_specs = (P(None, "dp", "section", None), P("section", "dp", None))
    return jax.shard_map(
        on_device, mesh=mesh, in_specs=in_specs, out_specs=out_specs, check_vma=False
    )
```

```python
import functools

import jax
import jax.numpy as jnp
from jax import lax
from jax.experimental import pallas as pl
from jax.experimental.pallas import tpu as pltpu
from jax.sharding import PartitionSpec as P

MESH = pl.DeviceIdType.MESH
F32, BF16 = jnp.float32, jnp.bfloat16
HALVES = 2
CHUNKS = 2


def tiles_of(total, most):
    size = min(total, most)
    return size, total // size


def kernel(
    n_sec,
    n_dp,
    x_hbm,
    inc_hbm,
    adj_hbm,
    obj_hbm,
    kept_hbm,
    w_hbm,
    ahead_hbm,
    grads_hbm,
    w,
    x4,
    c4,
    k4,
    n4,
    p4,
    h4,
    o6,
    fn,
    fh,
    inv_ref,
    g_ref,
    part_send,
    part_recv,
    own,
    y_send,
    y_recv,
    grad_out,
    local_sem,
    w_send,
    w_recv,
    mir_send,
    mir_recv,
    pass_send,
    pass_recv,
    red_send,
    red_recv,
    out_sem,
):
    s = lax.axis_index("section")
    r = lax.axis_index("dp")
    groups = n_dp // 2
    h, c = r // 2, r % 2
    partner = 2 * h + (1 - c)
    opposite = n_sec - 1 - s
    first, last = s == 0, s == n_sec - 1
    rows = w_hbm.shape[1]
    width = w_hbm.shape[2]
    ff = width // 3
    tokens, features = x_hbm.shape[2], x_hbm.shape[3]

    def remote(src, dst, send, recv, **where):
        return pltpu.make_async_remote_copy(
            src_ref=src,
            dst_ref=dst,
            send_sem=send,
            recv_sem=recv,
            device_id=where,
            device_id_type=MESH,
        )

    def dp_at(j):
        return 2 * lax.rem(h + j, groups) + c

    def span(block, size=tokens):
        return pl.ds(block * size, size)

    barrier = pltpu.get_barrier_semaphore()

    def greet(**where):
        pl.semaphore_signal(barrier, inc=1, device_id=where, device_id_type=MESH)

    greet(section=opposite)
    greet(dp=partner)
    for j in range(1, groups):
        greet(dp=dp_at(j))

    greet(section=lax.rem(s + 1, n_sec))
    greet(section=lax.rem(s + n_sec - 1, n_sec))

    local = [
        pltpu.make_async_copy(w_hbm.at[0], w.at[pl.ds(pl.multiple_of(r * rows, rows), rows)], local_sem.at[0]),
        pltpu.make_async_copy(kept_hbm.at[0, 0, 0], k4.at[span(0)], local_sem.at[1]),
        pltpu.make_async_copy(adj_hbm.at[0, 0], c4.at[span(0)], local_sem.at[2]),
        pltpu.make_async_copy(x_hbm.at[0, 0], x4.at[span(0)], local_sem.at[3]),
        pltpu.make_async_copy(kept_hbm.at[0, 1, 0], k4.at[span(2)], local_sem.at[4]),
    ]
    for copy in local:
        copy.start()
    edge_in = [
        pltpu.make_async_copy(inc_hbm.at[d, 0], x4.at[span(2 + d)], local_sem.at[5 + d])
        for d in range(2)
    ]
    edge_cot = [
        pltpu.make_async_copy(obj_hbm.at[d, 0], c4.at[span(2 + d)], local_sem.at[7 + d])
        for d in range(2)
    ]

    @pl.when(first)
    def _():
        for copy in edge_in:
            copy.start()

    @pl.when(last)
    def _():
        for copy in edge_cot:
            copy.start()

    pl.semaphore_wait(barrier, 4 + (groups - 1))

    piece = rows // CHUNKS

    def w_rows(owner, k):
        return w.at[pl.ds(pl.multiple_of(owner * rows + k * piece, piece), piece)]

    outgoing = []
    for k in range(CHUNKS):
        for j in range(1, groups):
            copy = remote(
                w_hbm.at[0, pl.ds(k * piece, piece)],
                w_rows(r, k),
                w_send.at[0, j, k],
                w_recv.at[0, j, k],
                dp=dp_at(j),
            )
            copy.start()
            outgoing.append(copy)

    mirror_first = [
        (kept_hbm.at[1, 0, 0], k4.at[span(1)]),
        (adj_hbm.at[1, 0], c4.at[span(1)]),
        (kept_hbm.at[1, 1, 0], k4.at[span(3)]),
    ]
    mirror = [
        remote(src, dst, mir_send.at[i], mir_recv.at[i], section=opposite)
        for i, (src, dst) in enumerate(mirror_first)
    ]
    for copy in mirror:
        copy.start()
    for k in range(CHUNKS):
        copy = remote(
            w_hbm.at[0, pl.ds(k * piece, piece)],
            w_rows(r, k),
            w_send.at[1, 0, k],
            w_recv.at[1, 0, k],
            dp=partner,
        )
        copy.start()
        outgoing.append(copy)
    for k in range(CHUNKS):
        for j in range(1, groups):
            source = 2 * lax.rem(h + groups - j, groups) + c
            arrived = w_rows(source, k)
            remote(arrived, arrived, w_send.at[0, j, k], w_recv.at[0, j, k], dp=source).wait_recv()
            copy = remote(
                arrived, arrived, w_send.at[1, j, k], w_recv.at[1, j, k], dp=partner
            )
            copy.start()
            outgoing.append(copy)
    for copy in local:
        copy.wait()
    for k in range(CHUNKS):
        for j in range(groups):
            source = 2 * lax.rem(h + groups - j, groups) + (1 - c)
            arrived = w_rows(source, k)
            remote(arrived, arrived, w_send.at[1, j, k], w_recv.at[1, j, k], dp=partner).wait_recv()

    col, f_tiles = tiles_of(ff, 256)
    wide, h_tiles = tiles_of(features, 256)

    def normalize(src, start, count, dst, dst_start, keep):
        step = 16

        def body(i, carry):
            at = pl.ds(pl.multiple_of(start + i * step, step), step)
            to = pl.ds(pl.multiple_of(dst_start + i * step, step), step)
            values = src[at, :].astype(F32)
            inverse = lax.rsqrt(jnp.mean(values * values, axis=-1, keepdims=True) + 1e-06)
            dst[to, :] = (values * inverse).astype(BF16)
            if keep:
                inv_ref[pl.ds(pl.multiple_of(i * step, step), step), :] = inverse
            return carry

        lax.fori_loop(0, count // step, body, 0)

    def dot(a, b):
        return jnp.dot(a, b, preferred_element_type=F32)

    def dot_t(a, b):
        return lax.dot_general(a, b, (((1,), (1,)), ((), ())), preferred_element_type=F32)

    def forward(start, count, out_start):
        at = pl.ds(start, count)
        normalize(x4, start, count, fn, 0, False)
        here = pl.ds(0, count)

        def up(j, carry):
            gate_part = dot(fn[here, :], w[:, pl.ds(pl.multiple_of(j * col, col), col)])
            up_part = dot(fn[here, :], w[:, pl.ds(pl.multiple_of(ff + j * col, col), col)])
            fh[here, pl.ds(pl.multiple_of(j * col, col), col)] = (
                gate_part * jax.nn.sigmoid(gate_part) * up_part
            ).astype(BF16)
            return carry

        lax.fori_loop(0, f_tiles, up, 0)

        def down(j, carry):
            lanes = pl.ds(pl.multiple_of(j * wide, wide), wide)
            branch = dot_t(fh[here, :], w[lanes, 2 * ff :])
            o6[pl.ds(out_start, count), lanes] = (x4[at, lanes].astype(F32) + branch).astype(BF16)
            return carry

        lax.fori_loop(0, h_tiles, down, 0)

    def reverse(slot, out_slot):
        at = span(slot)
        normalize(k4, slot * tokens, tokens, n4, slot * tokens, True)

        def up(j, carry):
            lanes = pl.ds(pl.multiple_of(j * col, col), col)
            beyond = pl.ds(pl.multiple_of(ff + j * col, col), col)
            gate_part = dot(n4[at, :], w[:, lanes])
            up_part = dot(n4[at, :], w[:, beyond])
            hidden_grad = dot(c4[at, :], w[:, pl.ds(pl.multiple_of(2 * ff + j * col, col), col)])
            sigmoid_gate = jax.nn.sigmoid(gate_part)
            silu_gate = gate_part * sigmoid_gate
            h4[at, lanes] = (silu_gate * up_part).astype(BF16)
            p4[at, lanes] = (
                hidden_grad * up_part * sigmoid_gate * (1.0 + gate_part * (1.0 - sigmoid_gate))
            ).astype(BF16)
            p4[at, beyond] = (hidden_grad * silu_gate).astype(BF16)
            return carry

        lax.fori_loop(0, f_tiles, up, 0)
        if out_slot is None:
            return

        def back(j, total):
            lanes = pl.ds(pl.multiple_of(j * wide, wide), wide)
            grad = dot_t(p4[at, :], w[lanes, : 2 * ff])
            g_ref[:, lanes] = grad
            return total + jnp.sum(grad * k4[at, lanes].astype(F32), axis=-1, keepdims=True)

        total = lax.fori_loop(0, h_tiles, back, jnp.zeros((tokens, 1), F32))
        inverse = inv_ref[...]
        scale = inverse * inverse * inverse * (total / features)

        def finish(j, carry):
            lanes = pl.ds(pl.multiple_of(j * wide, wide), wide)
            o6[span(out_slot), lanes] = (
                c4[at, lanes].astype(F32)
                + inverse * g_ref[:, lanes]
                - k4[at, lanes].astype(F32) * scale
            ).astype(BF16)
            return carry

        lax.fori_loop(0, h_tiles, finish, 0)

    def weight_rows(q, store):
        size, count = tiles_of(rows, 256)
        for t in range(count):
            lanes = pl.ds(pl.multiple_of(q * rows + t * size, size), size)
            left, left_cot = n4[:, lanes], c4[:, lanes]
            across = (((0,), (0,)), ((), ()))

            def inward(j, carry):
                out = pl.ds(pl.multiple_of(j * col, col), col)
                store(
                    pl.ds(t * size, size),
                    out,
                    lax.dot_general(left, p4[:, out], across, preferred_element_type=F32),
                )
                return carry

            lax.fori_loop(0, 2 * f_tiles, inward, 0)

            def outward(j, carry):
                lanes_in = pl.ds(pl.multiple_of(j * col, col), col)
                out = pl.ds(pl.multiple_of(2 * ff + j * col, col), col)
                store(
                    pl.ds(t * size, size),
                    out,
                    lax.dot_general(left_cot, h4[:, lanes_in], across, preferred_element_type=F32),
                )
                return carry

            lax.fori_loop(0, f_tiles, outward, 0)

    def send_pass(i, src, dst, step):
        to = s + step
        copy = remote(src, dst, pass_send.at[i], pass_recv.at[i], section=to)
        inside = s < n_sec - 1 if step > 0 else s > 0

        @pl.when(inside)
        def _():
            copy.start()

    def recv_pass(i, dst, step, edge):
        outside = first if step > 0 else last
        copy = remote(dst, dst, pass_send.at[i], pass_recv.at[i], section=s)

        @pl.when(jnp.logical_not(outside))
        def _():
            copy.wait_recv()

        if edge is not None:

            @pl.when(outside)
            def _():
                edge.wait()

    half = tokens // HALVES
    reverse(0, 2)
    send_pass(0, o6.at[span(2)], c4.at[span(2)], -1)
    forward(0, tokens, 0)
    send_pass(2, o6.at[span(0)], x4.at[span(2)], 1)
    mirror[0].wait_recv()
    mirror[1].wait_recv()
    reverse(1, 3)
    send_pass(1, o6.at[span(3)], c4.at[span(3)], -1)
    mirror_x = []
    for i in range(HALVES):
        copy = remote(
            x_hbm.at[1, 0, pl.ds(i * half, half)],
            x4.at[pl.ds(tokens + i * half, half)],
            mir_send.at[3 + i],
            mir_recv.at[3 + i],
            section=opposite,
        )
        copy.start()
        mirror_x.append(copy)
    recv_pass(2, x4.at[span(2)], 1, edge_in[0])
    forward(2 * tokens, tokens, 4 * tokens)
    down_out = pltpu.make_async_copy(o6.at[span(4)], ahead_hbm.at[0, 0], out_sem.at[0])
    down_out.start()
    recv_pass(0, c4.at[span(2)], -1, edge_cot[0])
    reverse(2, None)
    mirror[2].wait_recv()
    recv_pass(1, c4.at[span(3)], -1, edge_cot[1])
    reverse(3, None)

    reduce_copies = []
    for j in range(groups):
        g = lax.rem(h + j, groups)

        def to_partner(at, lanes, value, j=j):
            part_send[j, at, lanes] = value.astype(BF16)

        weight_rows(2 * g + (1 - c), to_partner)
        copy = remote(
            part_send.at[j], part_recv.at[j], red_send.at[0, j], red_recv.at[0, j], dp=partner
        )
        copy.start()
        reduce_copies.append(copy)
    step, count = tiles_of(rows, 32)
    for j in list(range(1, groups)) + [0]:
        g = lax.rem(h + j, groups)

        def to_own(at, lanes, value, j=j):
            own[j, at, lanes] = value

        weight_rows(2 * g + c, to_own)
    for j in range(1, groups):
        reduce_copies[j].wait_recv()

        def add(i, carry, j=j):
            at = pl.ds(pl.multiple_of(i * step, step), step)
            y_send[j - 1, at, :] = (own[j, at, :] + part_recv[j, at, :].astype(F32)).astype(BF16)
            return carry

        lax.fori_loop(0, count, add, 0)
        copy = remote(
            y_send.at[j - 1], y_recv.at[j - 1], red_send.at[1, j], red_recv.at[1, j], dp=dp_at(j)
        )
        copy.start()
        reduce_copies.append(copy)
    for i in range(HALVES):
        mirror_x[i].wait_recv()
        forward(tokens + i * half, half, tokens + i * half)
        send_pass(
            3 + i,
            o6.at[pl.ds(tokens + i * half, half)],
            x4.at[pl.ds(3 * tokens + i * half, half)],
            1,
        )
    returned = []
    for i in range(HALVES):
        recv_pass(
            3 + i, x4.at[pl.ds(3 * tokens + i * half, half)], 1, edge_in[1] if i == 0 else None
        )
        forward(3 * tokens + i * half, half, 5 * tokens + i * half)
        copy = remote(
            o6.at[pl.ds(5 * tokens + i * half, half)],
            ahead_hbm.at[1, 0, pl.ds(i * half, half)],
            mir_send.at[3 + HALVES + i],
            mir_recv.at[3 + HALVES + i],
            section=opposite,
        )
        copy.start()
        returned.append(copy)
    reduce_copies[0].wait_recv()
    for copy in reduce_copies[groups:]:
        copy.wait_recv()

    def final(i, carry):
        at = pl.ds(pl.multiple_of(i * step, step), step)
        total = own[0, at, :] + part_recv[0, at, :].astype(F32)
        for j in range(1, groups):
            total = total + y_recv[j - 1, at, :].astype(F32)
        grad_out[at, :] = total
        return carry

    lax.fori_loop(0, count, final, 0)
    grad_copy = pltpu.make_async_copy(grad_out, grads_hbm.at[0], out_sem.at[1])
    grad_copy.start()
    for copy in returned:
        copy.wait_recv()

    for copy in outgoing + mirror + mirror_x + returned + reduce_copies:
        copy.wait_send()

    def drain(i, size, step):
        inside = s < n_sec - 1 if step > 0 else s > 0
        view = o6.at[pl.ds(0, size)]

        @pl.when(inside)
        def _():
            remote(view, view, pass_send.at[i], pass_recv.at[i], section=s).wait_send()

    drain(0, tokens, -1)
    drain(1, tokens, -1)
    drain(2, tokens, 1)
    for i in range(HALVES):
        drain(3 + i, half, 1)
    down_out.wait()
    grad_copy.wait()


def on_device(n_sec, n_dp, *arrays):
    x, inc, adj, obj, kept, weights = arrays
    _, _, tokens, features = x.shape
    _, rows, width = weights.shape
    ff, groups = width // 3, n_dp // 2
    dma = pltpu.SemaphoreType.DMA
    anywhere = pl.BlockSpec(memory_space=pl.ANY)
    return pl.pallas_call(
        functools.partial(kernel, n_sec, n_dp),
        out_shape=(
            jax.ShapeDtypeStruct(x.shape, BF16),
            jax.ShapeDtypeStruct(weights.shape, F32),
        ),
        in_specs=[anywhere] * 6,
        out_specs=(anywhere, anywhere),
        scratch_shapes=[
            pltpu.VMEM((features, width), BF16),
            pltpu.VMEM((4 * tokens, features), BF16),
            pltpu.VMEM((4 * tokens, features), BF16),
            pltpu.VMEM((4 * tokens, features), BF16),
            pltpu.VMEM((4 * tokens, features), BF16),
            pltpu.VMEM((4 * tokens, 2 * ff), BF16),
            pltpu.VMEM((4 * tokens, ff), BF16),
            pltpu.VMEM((6 * tokens, features), BF16),
            pltpu.VMEM((tokens, features), BF16),
            pltpu.VMEM((tokens, ff), BF16),
            pltpu.VMEM((tokens, 1), F32),
            pltpu.VMEM((tokens, features), F32),
            pltpu.VMEM((groups, rows, width), BF16),
            pltpu.VMEM((groups, rows, width), BF16),
            pltpu.VMEM((groups, rows, width), F32),
            pltpu.VMEM((groups - 1, rows, width), BF16),
            pltpu.VMEM((groups - 1, rows, width), BF16),
            pltpu.VMEM((rows, width), F32),
            dma((9,)),
            dma((2, groups, CHUNKS)),
            dma((2, groups, CHUNKS)),
            dma((3 + 2 * HALVES,)),
            dma((3 + 2 * HALVES,)),
            dma((3 + HALVES,)),
            dma((3 + HALVES,)),
            dma((2, groups)),
            dma((2, groups)),
            dma((2,)),
        ],
        compiler_params=pltpu.CompilerParams(
            collective_id=0, has_side_effects=True, vmem_limit_bytes=60 * 1024 * 1024
        ),
    )(x, inc, adj, obj, kept, weights)


def solution(mesh):
    in_specs = (
        P(None, "dp", "section", None),
        P(None, "dp", None, None),
        P(None, "dp", "section", None),
        P(None, "dp", None, None),
        P(None, None, "dp", "section", None),
        P("section", "dp", None),
    )
    out_specs = (P(None, "dp", "section", None), P("section", "dp", None))
    body = functools.partial(on_device, mesh.shape["section"], mesh.shape["dp"])
    return jax.shard_map(
        body, mesh=mesh, in_specs=in_specs, out_specs=out_specs, check_vma=False
    )
```

```python
import functools

import jax
import jax.numpy as jnp
from jax import lax
from jax.experimental import pallas as pl
from jax.experimental.pallas import tpu as pltpu
from jax.sharding import PartitionSpec as P

MESH = pl.DeviceIdType.MESH
F32, BF16 = jnp.float32, jnp.bfloat16
HALVES = 2
CHUNKS = 2


def tiles_of(total, most):
    size = min(total, most)
    return size, total // size


def kernel(
    n_sec,
    n_dp,
    x_hbm,
    inc_hbm,
    adj_hbm,
    obj_hbm,
    kept_hbm,
    w_hbm,
    ahead_hbm,
    grads_hbm,
    w,
    x4,
    c4,
    k4,
    n4,
    p4,
    h4,
    o6,
    fn,
    fh,
    inv_ref,
    g_ref,
    part_send,
    part_recv,
    own,
    y_send,
    y_recv,
    grad_out,
    local_sem,
    w_send,
    w_recv,
    mir_send,
    mir_recv,
    pass_send,
    pass_recv,
    red_send,
    red_recv,
    out_sem,
):
    s = lax.axis_index("section")
    r = lax.axis_index("dp")
    groups = n_dp // 2
    h, c = r // 2, r % 2
    partner = 2 * h + (1 - c)
    opposite = n_sec - 1 - s
    first, last = s == 0, s == n_sec - 1
    rows = w_hbm.shape[1]
    width = w_hbm.shape[2]
    ff = width // 3
    tokens, features = x_hbm.shape[2], x_hbm.shape[3]

    def remote(src, dst, send, recv, **where):
        return pltpu.make_async_remote_copy(
            src_ref=src,
            dst_ref=dst,
            send_sem=send,
            recv_sem=recv,
            device_id=where,
            device_id_type=MESH,
        )

    def dp_at(j):
        return 2 * lax.rem(h + j, groups) + c

    def span(block, size=tokens):
        return pl.ds(block * size, size)

    half = tokens // HALVES

    barrier = pltpu.get_barrier_semaphore()

    def greet(**where):
        pl.semaphore_signal(barrier, inc=1, device_id=where, device_id_type=MESH)

    greet(section=opposite)
    greet(dp=partner)
    for j in range(1, groups):
        greet(dp=dp_at(j))

    greet(section=lax.rem(s + 1, n_sec))
    greet(section=lax.rem(s + n_sec - 1, n_sec))

    local = [
        pltpu.make_async_copy(w_hbm.at[0], w.at[pl.ds(pl.multiple_of(r * rows, rows), rows)], local_sem.at[0]),
        pltpu.make_async_copy(kept_hbm.at[0, 0, 0], k4.at[span(0)], local_sem.at[1]),
        pltpu.make_async_copy(adj_hbm.at[0, 0], c4.at[span(0)], local_sem.at[2]),
        pltpu.make_async_copy(x_hbm.at[0, 0], x4.at[span(0)], local_sem.at[3]),
        pltpu.make_async_copy(kept_hbm.at[0, 1, 0], k4.at[span(2)], local_sem.at[4]),
    ]
    for copy in local:
        copy.start()
    edge_in = [
        pltpu.make_async_copy(inc_hbm.at[d, 0], x4.at[span(2 + d)], local_sem.at[5 + d])
        for d in range(2)
    ]
    edge_cot = [
        pltpu.make_async_copy(obj_hbm.at[d, 0], c4.at[span(2 + d)], local_sem.at[7 + d])
        for d in range(2)
    ]

    @pl.when(first)
    def _():
        for copy in edge_in:
            copy.start()

    @pl.when(last)
    def _():
        for copy in edge_cot:
            copy.start()

    pl.semaphore_wait(barrier, 4 + (groups - 1))

    piece = rows // CHUNKS

    def w_rows(owner, k):
        return w.at[pl.ds(pl.multiple_of(owner * rows + k * piece, piece), piece)]

    outgoing = []
    for k in range(CHUNKS):
        for j in range(1, groups):
            copy = remote(
                w_hbm.at[0, pl.ds(k * piece, piece)],
                w_rows(r, k),
                w_send.at[0, j, k],
                w_recv.at[0, j, k],
                dp=dp_at(j),
            )
            copy.start()
            outgoing.append(copy)

    mirror_first = [
        (kept_hbm.at[1, 0, 0], k4.at[span(1)]),
        (adj_hbm.at[1, 0], c4.at[span(1)]),
        (kept_hbm.at[1, 1, 0], k4.at[span(3)]),
    ]
    mirror = [
        remote(src, dst, mir_send.at[i], mir_recv.at[i], section=opposite)
        for i, (src, dst) in enumerate(mirror_first)
    ]
    for copy in mirror:
        copy.start()
    for k in range(CHUNKS):
        copy = remote(
            w_hbm.at[0, pl.ds(k * piece, piece)],
            w_rows(r, k),
            w_send.at[1, 0, k],
            w_recv.at[1, 0, k],
            dp=partner,
        )
        copy.start()
        outgoing.append(copy)
    for k in range(CHUNKS):
        for j in range(1, groups):
            source = 2 * lax.rem(h + groups - j, groups) + c
            arrived = w_rows(source, k)
            remote(arrived, arrived, w_send.at[0, j, k], w_recv.at[0, j, k], dp=source).wait_recv()
            copy = remote(
                arrived, arrived, w_send.at[1, j, k], w_recv.at[1, j, k], dp=partner
            )
            copy.start()
            outgoing.append(copy)
    for copy in local:
        copy.wait()
    for k in range(CHUNKS):
        for j in range(groups):
            source = 2 * lax.rem(h + groups - j, groups) + (1 - c)
            arrived = w_rows(source, k)
            remote(arrived, arrived, w_send.at[1, j, k], w_recv.at[1, j, k], dp=partner).wait_recv()

    col, f_tiles = tiles_of(ff, 256)
    wide, h_tiles = tiles_of(features, 256)

    def normalize(src, start, count, dst, dst_start, keep):
        step = 16

        def body(i, carry):
            at = pl.ds(pl.multiple_of(start + i * step, step), step)
            to = pl.ds(pl.multiple_of(dst_start + i * step, step), step)
            values = src[at, :].astype(F32)
            inverse = lax.rsqrt(jnp.mean(values * values, axis=-1, keepdims=True) + 1e-06)
            dst[to, :] = (values * inverse).astype(BF16)
            if keep:
                inv_ref[pl.ds(pl.multiple_of(i * step, step), step), :] = inverse
            return carry

        lax.fori_loop(0, count // step, body, 0)

    def dot(a, b):
        return jnp.dot(a, b, preferred_element_type=F32)

    def dot_t(a, b):
        return lax.dot_general(a, b, (((1,), (1,)), ((), ())), preferred_element_type=F32)

    def forward(start, count, out_start):
        at = pl.ds(start, count)
        normalize(x4, start, count, fn, 0, False)
        here = pl.ds(0, count)

        def up(j, carry):
            gate_part = dot(fn[here, :], w[:, pl.ds(pl.multiple_of(j * col, col), col)])
            up_part = dot(fn[here, :], w[:, pl.ds(pl.multiple_of(ff + j * col, col), col)])
            fh[here, pl.ds(pl.multiple_of(j * col, col), col)] = (
                gate_part * jax.nn.sigmoid(gate_part) * up_part
            ).astype(BF16)
            return carry

        lax.fori_loop(0, f_tiles, up, 0)

        def down(j, carry):
            lanes = pl.ds(pl.multiple_of(j * wide, wide), wide)
            branch = dot_t(fh[here, :], w[lanes, 2 * ff :])
            o6[pl.ds(out_start, count), lanes] = (x4[at, lanes].astype(F32) + branch).astype(BF16)
            return carry

        lax.fori_loop(0, h_tiles, down, 0)

    def reverse(slot, out_slot):
        at = span(slot)
        normalize(k4, slot * tokens, tokens, n4, slot * tokens, True)

        def up(j, carry):
            lanes = pl.ds(pl.multiple_of(j * col, col), col)
            beyond = pl.ds(pl.multiple_of(ff + j * col, col), col)
            gate_part = dot(n4[at, :], w[:, lanes])
            up_part = dot(n4[at, :], w[:, beyond])
            hidden_grad = dot(c4[at, :], w[:, pl.ds(pl.multiple_of(2 * ff + j * col, col), col)])
            sigmoid_gate = jax.nn.sigmoid(gate_part)
            silu_gate = gate_part * sigmoid_gate
            h4[at, lanes] = (silu_gate * up_part).astype(BF16)
            p4[at, lanes] = (
                hidden_grad * up_part * sigmoid_gate * (1.0 + gate_part * (1.0 - sigmoid_gate))
            ).astype(BF16)
            p4[at, beyond] = (hidden_grad * silu_gate).astype(BF16)
            return carry

        lax.fori_loop(0, f_tiles, up, 0)
        if out_slot is None:
            return

        def back(j, total):
            lanes = pl.ds(pl.multiple_of(j * wide, wide), wide)
            grad = dot_t(p4[at, :], w[lanes, : 2 * ff])
            g_ref[:, lanes] = grad
            return total + jnp.sum(grad * k4[at, lanes].astype(F32), axis=-1, keepdims=True)

        total = lax.fori_loop(0, h_tiles, back, jnp.zeros((tokens, 1), F32))
        inverse = inv_ref[...]
        scale = inverse * inverse * inverse * (total / features)

        def finish(j, carry):
            lanes = pl.ds(pl.multiple_of(j * wide, wide), wide)
            o6[span(out_slot), lanes] = (
                c4[at, lanes].astype(F32)
                + inverse * g_ref[:, lanes]
                - k4[at, lanes].astype(F32) * scale
            ).astype(BF16)
            return carry

        lax.fori_loop(0, h_tiles, finish, 0)

    def weight_rows(q, store):
        size, count = tiles_of(rows, 256)
        for t in range(count):
            lanes = pl.ds(pl.multiple_of(q * rows + t * size, size), size)
            left, left_cot = n4[:, lanes], c4[:, lanes]
            across = (((0,), (0,)), ((), ()))

            def inward(j, carry):
                out = pl.ds(pl.multiple_of(j * col, col), col)
                store(
                    pl.ds(t * size, size),
                    out,
                    lax.dot_general(left, p4[:, out], across, preferred_element_type=F32),
                )
                return carry

            lax.fori_loop(0, 2 * f_tiles, inward, 0)

            def outward(j, carry):
                lanes_in = pl.ds(pl.multiple_of(j * col, col), col)
                out = pl.ds(pl.multiple_of(2 * ff + j * col, col), col)
                store(
                    pl.ds(t * size, size),
                    out,
                    lax.dot_general(left_cot, h4[:, lanes_in], across, preferred_element_type=F32),
                )
                return carry

            lax.fori_loop(0, f_tiles, outward, 0)

    def send_pass(i, src, dst, step):
        to = s + step
        copy = remote(src, dst, pass_send.at[i], pass_recv.at[i], section=to)
        inside = s < n_sec - 1 if step > 0 else s > 0

        @pl.when(inside)
        def _():
            copy.start()

    def recv_pass(i, dst, step, edge):
        outside = first if step > 0 else last
        copy = remote(dst, dst, pass_send.at[i], pass_recv.at[i], section=s)

        @pl.when(jnp.logical_not(outside))
        def _():
            copy.wait_recv()

        if edge is not None:

            @pl.when(outside)
            def _():
                edge.wait()

    reverse(0, 2)
    send_pass(0, o6.at[span(2)], c4.at[span(2)], -1)
    forward(0, tokens, 0)
    send_pass(2, o6.at[span(0)], x4.at[span(2)], 1)
    mirror[0].wait_recv()
    mirror[1].wait_recv()
    reverse(1, 3)
    send_pass(1, o6.at[span(3)], c4.at[span(3)], -1)
    recv_pass(2, x4.at[span(2)], 1, edge_in[0])
    forward(2 * tokens, tokens, 4 * tokens)
    down_out = pltpu.make_async_copy(o6.at[span(4)], ahead_hbm.at[0, 0], out_sem.at[0])
    down_out.start()
    recv_pass(0, c4.at[span(2)], -1, edge_cot[0])
    reverse(2, None)
    mirror[2].wait_recv()
    mirror_x = []
    for i in range(HALVES):
        copy = remote(
            x_hbm.at[1, 0, pl.ds(i * half, half)],
            x4.at[pl.ds(tokens + i * half, half)],
            mir_send.at[3 + i],
            mir_recv.at[3 + i],
            section=opposite,
        )
        copy.start()
        mirror_x.append(copy)
    recv_pass(1, c4.at[span(3)], -1, edge_cot[1])
    reverse(3, None)

    reduce_copies = [None] * groups
    for j in list(range(1, groups)) + [0]:
        g = lax.rem(h + j, groups)

        def to_partner(at, lanes, value, j=j):
            part_send[j, at, lanes] = value.astype(BF16)

        weight_rows(2 * g + (1 - c), to_partner)
        copy = remote(
            part_send.at[j], part_recv.at[j], red_send.at[0, j], red_recv.at[0, j], dp=partner
        )
        copy.start()
        reduce_copies[j] = copy
    step, count = tiles_of(rows, 32)
    for j in list(range(1, groups)) + [0]:
        g = lax.rem(h + j, groups)

        def to_own(at, lanes, value, j=j):
            own[j, at, lanes] = value

        weight_rows(2 * g + c, to_own)
    for j in range(1, groups):
        reduce_copies[j].wait_recv()

        def add(i, carry, j=j):
            at = pl.ds(pl.multiple_of(i * step, step), step)
            y_send[j - 1, at, :] = (own[j, at, :] + part_recv[j, at, :].astype(F32)).astype(BF16)
            return carry

        lax.fori_loop(0, count, add, 0)
        copy = remote(
            y_send.at[j - 1], y_recv.at[j - 1], red_send.at[1, j], red_recv.at[1, j], dp=dp_at(j)
        )
        copy.start()
        reduce_copies.append(copy)
    for i in range(HALVES):
        mirror_x[i].wait_recv()
        forward(tokens + i * half, half, tokens + i * half)
        send_pass(
            3 + i,
            o6.at[pl.ds(tokens + i * half, half)],
            x4.at[pl.ds(3 * tokens + i * half, half)],
            1,
        )
    returned = []
    for i in range(HALVES):
        recv_pass(
            3 + i, x4.at[pl.ds(3 * tokens + i * half, half)], 1, edge_in[1] if i == 0 else None
        )
        forward(3 * tokens + i * half, half, 5 * tokens + i * half)
        copy = remote(
            o6.at[pl.ds(5 * tokens + i * half, half)],
            ahead_hbm.at[1, 0, pl.ds(i * half, half)],
            mir_send.at[3 + HALVES + i],
            mir_recv.at[3 + HALVES + i],
            section=opposite,
        )
        copy.start()
        returned.append(copy)
    reduce_copies[0].wait_recv()
    for copy in reduce_copies[groups:]:
        copy.wait_recv()

    def final(i, carry):
        at = pl.ds(pl.multiple_of(i * step, step), step)
        total = own[0, at, :] + part_recv[0, at, :].astype(F32)
        for j in range(1, groups):
            total = total + y_recv[j - 1, at, :].astype(F32)
        grad_out[at, :] = total
        return carry

    lax.fori_loop(0, count, final, 0)
    grad_copy = pltpu.make_async_copy(grad_out, grads_hbm.at[0], out_sem.at[1])
    grad_copy.start()
    for copy in returned:
        copy.wait_recv()

    for copy in outgoing + mirror + mirror_x + returned + reduce_copies:
        copy.wait_send()

    def drain(i, size, step):
        inside = s < n_sec - 1 if step > 0 else s > 0
        view = o6.at[pl.ds(0, size)]

        @pl.when(inside)
        def _():
            remote(view, view, pass_send.at[i], pass_recv.at[i], section=s).wait_send()

    drain(0, tokens, -1)
    drain(1, tokens, -1)
    drain(2, tokens, 1)
    for i in range(HALVES):
        drain(3 + i, half, 1)
    down_out.wait()
    grad_copy.wait()


def on_device(n_sec, n_dp, *arrays):
    x, inc, adj, obj, kept, weights = arrays
    _, _, tokens, features = x.shape
    _, rows, width = weights.shape
    ff, groups = width // 3, n_dp // 2
    dma = pltpu.SemaphoreType.DMA
    anywhere = pl.BlockSpec(memory_space=pl.ANY)
    return pl.pallas_call(
        functools.partial(kernel, n_sec, n_dp),
        out_shape=(
            jax.ShapeDtypeStruct(x.shape, BF16),
            jax.ShapeDtypeStruct(weights.shape, F32),
        ),
        in_specs=[anywhere] * 6,
        out_specs=(anywhere, anywhere),
        scratch_shapes=[
            pltpu.VMEM((features, width), BF16),
            pltpu.VMEM((4 * tokens, features), BF16),
            pltpu.VMEM((4 * tokens, features), BF16),
            pltpu.VMEM((4 * tokens, features), BF16),
            pltpu.VMEM((4 * tokens, features), BF16),
            pltpu.VMEM((4 * tokens, 2 * ff), BF16),
            pltpu.VMEM((4 * tokens, ff), BF16),
            pltpu.VMEM((6 * tokens, features), BF16),
            pltpu.VMEM((tokens, features), BF16),
            pltpu.VMEM((tokens, ff), BF16),
            pltpu.VMEM((tokens, 1), F32),
            pltpu.VMEM((tokens, features), F32),
            pltpu.VMEM((groups, rows, width), BF16),
            pltpu.VMEM((groups, rows, width), BF16),
            pltpu.VMEM((groups, rows, width), F32),
            pltpu.VMEM((groups - 1, rows, width), BF16),
            pltpu.VMEM((groups - 1, rows, width), BF16),
            pltpu.VMEM((rows, width), F32),
            dma((9,)),
            dma((2, groups, CHUNKS)),
            dma((2, groups, CHUNKS)),
            dma((3 + 2 * HALVES,)),
            dma((3 + 2 * HALVES,)),
            dma((3 + HALVES,)),
            dma((3 + HALVES,)),
            dma((2, groups)),
            dma((2, groups)),
            dma((2,)),
        ],
        compiler_params=pltpu.CompilerParams(
            collective_id=0, has_side_effects=True, vmem_limit_bytes=60 * 1024 * 1024
        ),
    )(x, inc, adj, obj, kept, weights)


def solution(mesh):
    in_specs = (
        P(None, "dp", "section", None),
        P(None, "dp", None, None),
        P(None, "dp", "section", None),
        P(None, "dp", None, None),
        P(None, None, "dp", "section", None),
        P("section", "dp", None),
    )
    out_specs = (P(None, "dp", "section", None), P("section", "dp", None))
    body = functools.partial(on_device, mesh.shape["section"], mesh.shape["dp"])
    return jax.shard_map(
        body, mesh=mesh, in_specs=in_specs, out_specs=out_specs, check_vma=False
    )
```
